32 devices in a mesh: member: 2 (over x), space: 16 (over z, y, core).
Axes of the slice: x: 2, y: 2, z: 4, core: 2. Of those that a mesh axis runs over, the one named last changes fastest.
Arguments:
- node_states: bfloat16 [4096, 1024], P('space'), may hold values from -6 to 6
- noise: bfloat16 [2, 16, 4096], P('member', None, 'space'), may hold values from -4 to 4
- norm_gain: float32 [1024], replicated, may hold values from 0.5 to 1.5
- cond_weight: bfloat16 [16, 2048], replicated, may hold values from -1.5 to 1.5
- w_query: bfloat16 [1024, 1024], P('space'), may hold values from -0.1875 to 0.1875
- w_key: bfloat16 [1024, 1024], P('space'), may hold values from -0.1875 to 0.1875
- w_value: bfloat16 [1024, 1024], P('space'), may hold values from -0.1875 to 0.1875
- w_out: bfloat16 [1024, 1024], P('space'), may hold values from -0.1875 to 0.1875
- edge_src: int32 [8, 4096], P(None, 'space'), may hold values from 0 to 511, as said below
- send_rows: int32 [4096], P('space'), may hold values from 0 to 255, as said below
- dec_src: int32 [3, 16384], P(None, 'space'), may hold values from 0 to 255
- dec_weight: float32 [3, 16384], P(None, 'space'), may hold values from 0.2 to 1
- w_decode: bfloat16 [100, 1024], replicated, may hold values from -0.1875 to 0.1875
- truth: bfloat16 [100, 16384], P(None, 'space'), may hold values from -6 to 6
- area: float32 [16384], P('space'), may hold values from 0.1 to 3.5
Outputs:
- loss: float32 [], replicated
- field_grad: bfloat16 [2, 100, 16384], P('member', None, 'space')
The draws below stay inside these ranges and needn't reach their ends.
Inputs may be any that keep to these rules, and one draw needn't show every extreme that they name: `send_rows`: each block's 2 * 128 entries are distinct node indices within that block. `edge_src`: entries below 128 name a row of the previous block's halo rows, entries from 384 on a row of the next block's; of each such halo half only a leading part of at least 64 rows is named, its length varying by block, and in some block the whole half is named.
All inputs are finite; a program needn't handle non-finite values.
Results may differ from the reference program's by a relative error of at most 0.015.
Values may be sent and summed in bfloat16 or wider, within the bound.
No kernel may reach another device: no remote copies, remote signals or barrier semaphores. Data moves between devices by JAX's collectives and lax.ppermute only.
A program may use at most 64 MiB of HBM per device.

```python
import math
import jax
import jax.numpy as jnp
from jax import lax

H = 1024
HEADS = 16
NOISE = 16
VARS = 100
KNB = 8
DEC_K = 3
HALO = 128
NODE_DEV = 256
GRID_DEV = 1024
MEMBERS = 2
NODES = 4096
GRID = 16384


def live_counts(key):
    devices = NODES // NODE_DEV
    counts = jax.random.randint(jax.random.fold_in(key, 7), (2, devices), HALO // 2, HALO + 1)
    return counts.at[:, 0].set(HALO).astype(jnp.int32)


def draw_send_rows(key, part):
    devices = NODES // NODE_DEV
    subkeys = jax.random.split(jax.random.fold_in(key, 11), devices)

    def choose(subkey):
        return jax.random.permutation(subkey, NODE_DEV)[:2 * HALO]
    chosen = jax.vmap(choose)(subkeys)
    return chosen.reshape(-1).astype(jnp.int32)


def draw_edge_src(key, part):
    devices = NODES // NODE_DEV
    counts = live_counts(key)
    anchor = jax.random.fold_in(key, 13)
    shape = (KNB, devices, NODE_DEV)
    region = jax.random.randint(jax.random.fold_in(anchor, 1), shape, 0, 8)
    local_pick = jax.random.randint(jax.random.fold_in(anchor, 2), shape, 0, NODE_DEV)
    left_pick = jax.random.randint(jax.random.fold_in(anchor, 3), shape, 0, counts[0][None, :, None])
    right_pick = jax.random.randint(jax.random.fold_in(anchor, 4), shape, 0, counts[1][None, :, None])
    chosen = jnp.where(region < 6, HALO + local_pick, jnp.where(region == 6, left_pick, HALO + NODE_DEV + right_pick))
    return chosen.reshape(KNB, NODES).astype(jnp.int32)


def draw_area(key, part):
    position = (jnp.arange(GRID, dtype=jnp.int32) % GRID_DEV).astype(jnp.float32) / GRID_DEV
    anchor = jax.random.fold_in(key, 17)
    rough = jnp.exp(jax.random.uniform(anchor, (GRID,), jnp.float32, jnp.log(0.5), 0.0))
    return (0.25 * jnp.exp(position * jnp.log(8.0)) * rough).astype(jnp.float32)


def with_ends(array, stream_key, low, largest):
    index_at = [jax.random.randint(jax.random.fold_in(stream_key, axis), (), 0, length) for axis, length in enumerate(array.shape)]
    widest = array.shape.index(max(array.shape))
    beside = index_at[:widest] + [(index_at[widest] + 1) % array.shape[widest]] + index_at[widest + 1:]
    return array.at[tuple(index_at)].set(low).at[tuple(beside)].set(largest)


def level_of(key, shape, shards, low, largest):
    gain = 1.0
    for dim, parts in shards:
        heights = jax.random.uniform(jax.random.fold_in(jax.random.fold_in(key, 6), dim), (parts,), jnp.float32, low / len(shards), largest / len(shards))
        gain = gain * jnp.repeat(jnp.exp(heights), shape[dim] // parts).reshape((-1,) + (1,) * (len(shape) - 1 - dim))
    return gain


def centred(stream_key, shape, scale, reach, shards=(), kind=jnp.bfloat16):
    drawn = scale * jax.random.normal(stream_key, shape, jnp.float32)
    if shards:
        drawn = drawn * level_of(stream_key, shape, shards, -0.22, 0.18)
    return jnp.clip(drawn, -reach, reach).astype(kind)


def setup_inputs(seed: int = 0) -> dict:
    seeds = jax.random.split(jax.random.key(seed), 16)
    node_states = centred(seeds[0], (NODES, H), 1.0, 6.0, ((0, 16),))
    noise = centred(seeds[1], (MEMBERS, NOISE, NODES), 0.5, 4.0, ((0, 2), (2, 16)))
    norm_gain = jnp.clip(1.0 + 0.1 * jax.random.normal(seeds[2], (H,), jnp.float32), 0.5, 1.5)
    cond_weight = centred(seeds[3], (NOISE, 2 * H), NOISE ** -0.5, 1.5)
    w_query = centred(seeds[4], (H, H), H ** -0.5, 0.1875, ((0, 16),))
    w_key = centred(seeds[5], (H, H), H ** -0.5, 0.1875, ((0, 16),))
    w_value = centred(seeds[6], (H, H), H ** -0.5, 0.1875, ((0, 16),))
    w_out = centred(seeds[7], (H, H), H ** -0.5, 0.1875, ((0, 16),))
    edge_src = draw_edge_src(jax.random.fold_in(seeds[15], 71), 0)
    send_rows = draw_send_rows(jax.random.fold_in(seeds[15], 71), 0)
    dec_src = with_ends(jax.random.randint(seeds[10], (DEC_K, GRID), 0, NODE_DEV), jax.random.fold_in(seeds[10], 1), 0, NODE_DEV - 1).astype(jnp.int32)
    dec_weight = jnp.clip(jnp.exp(math.log(1.0) - 1.609438 * jax.random.uniform(seeds[11], (DEC_K, GRID), jnp.float32) ** level_of(seeds[11], (DEC_K, GRID), ((1, 16),), -0.2, 0.2)), 0.2, 1.0)
    w_decode = centred(seeds[12], (VARS, H), H ** -0.5, 0.1875)
    truth = centred(seeds[13], (VARS, GRID), 1.0, 6.0, ((1, 16),))
    area = draw_area(jax.random.fold_in(seeds[15], 71), 0)
    return dict(node_states=node_states, noise=noise, norm_gain=norm_gain, cond_weight=cond_weight, w_query=w_query, w_key=w_key, w_value=w_value, w_out=w_out, edge_src=edge_src, send_rows=send_rows, dec_src=dec_src, dec_weight=dec_weight, w_decode=w_decode, truth=truth, area=area)


SMOOTH = 0.25
EPS = 1e-05

def condition(states, noise_block, norm_gain, cond_weight):
    values = states.astype(jnp.float32)
    center = values - lax.optimization_barrier(jnp.mean(values, axis=1, keepdims=True))
    spread = lax.optimization_barrier(jnp.mean(center * center, axis=1, keepdims=True))
    normed = center * lax.rsqrt(spread + EPS)
    terms = lax.dot_general(noise_block, cond_weight, (((0,), (0,)), ((), ())), preferred_element_type=jnp.float32)
    model_width = states.shape[1]
    return (normed * norm_gain * (1.0 + terms[:, :model_width]) + terms[:, model_width:]).astype(jnp.bfloat16)

def attention(query_rows, key_ext, value_ext, sources):
    row_count, model_width = query_rows.shape
    head_size = model_width // HEADS
    factor = 1.0 / head_size ** 0.5
    query_wide = query_rows.astype(jnp.float32).reshape(row_count, HEADS, head_size)
    numerator = jnp.zeros((row_count, HEADS, head_size), jnp.float32)
    denominator = jnp.zeros((row_count, HEADS), jnp.float32)
    for slot_index in range(sources.shape[0]):
        picked = sources[slot_index]
        gathered_key = key_ext[picked].astype(jnp.float32).reshape(row_count, HEADS, head_size)
        weight = jnp.exp(lax.optimization_barrier(jnp.sum(query_wide * gathered_key, axis=2)) * factor)
        gathered_value = value_ext[picked].astype(jnp.float32).reshape(row_count, HEADS, head_size)
        numerator = numerator + weight[:, :, None] * gathered_value
        denominator = denominator + weight
    return (numerator / denominator[:, :, None]).reshape(row_count, model_width).astype(jnp.bfloat16)

def decode(processed, sources, dec_weight, w_decode):
    gathered = jnp.zeros((sources.shape[1], processed.shape[1]), jnp.float32)
    for neighbour in range(sources.shape[0]):
        gathered = gathered + dec_weight[neighbour][:, None] * processed[sources[neighbour]].astype(jnp.float32)
    return lax.dot_general(w_decode, gathered.astype(jnp.bfloat16), (((1,), (1,)), ((), ())), preferred_element_type=jnp.float32).astype(jnp.bfloat16)

def smooth_abs(difference):
    return jnp.sqrt(difference * difference + SMOOTH * SMOOTH)

def reference(node_states, noise, norm_gain, cond_weight, w_query, w_key, w_value, w_out, edge_src, send_rows, dec_src, dec_weight, w_decode, truth, area):
    devices = NODES // NODE_DEV
    send_table = send_rows.reshape(devices, 2 * HALO).astype(jnp.int32)
    node_base = (jnp.arange(devices, dtype=jnp.int32) * NODE_DEV).astype(jnp.int32)
    left_block = jnp.roll(send_table[:, HALO:] + node_base[:, None], 1, axis=0)
    right_block = jnp.roll(send_table[:, :HALO] + node_base[:, None], -1, axis=0)
    own_block = node_base[:, None] + jnp.arange(NODE_DEV, dtype=jnp.int32)[None, :]
    extended = jnp.concatenate((left_block, own_block, right_block), axis=1).astype(jnp.int32)
    local_edges = edge_src.reshape(KNB, devices, NODE_DEV).astype(jnp.int32)
    broad = jnp.broadcast_to(extended[None], (KNB, devices, NODE_DEV + 2 * HALO))
    global_edges = jnp.take_along_axis(broad, local_edges, axis=2).reshape(KNB, NODES).astype(jnp.int32)
    global_dec = (dec_src.reshape(DEC_K, devices, GRID_DEV) + node_base[None, :, None]).reshape(DEC_K, GRID).astype(jnp.int32)
    field_list = []
    for member_index in range(MEMBERS):
        hidden = condition(node_states, noise[member_index], norm_gain, cond_weight)
        query_rows = jnp.dot(hidden, w_query, preferred_element_type=jnp.float32).astype(jnp.bfloat16)
        key_rows = jnp.dot(hidden, w_key, preferred_element_type=jnp.float32).astype(jnp.bfloat16)
        value_rows = jnp.dot(hidden, w_value, preferred_element_type=jnp.float32).astype(jnp.bfloat16)
        attended = attention(query_rows, key_rows, value_rows, global_edges)
        update = jnp.dot(attended, w_out, preferred_element_type=jnp.float32)
        processed = (node_states.astype(jnp.float32) + update).astype(jnp.bfloat16)
        field_list.append(decode(processed, global_dec, dec_weight, w_decode))
    values = jnp.stack(field_list).astype(jnp.float32)
    members = MEMBERS
    truth_wide = truth.astype(jnp.float32)
    skill_gap = values - truth_wide[None]
    skill_abs = smooth_abs(skill_gap)
    spread_abs = jnp.zeros_like(values)
    spread_slope = jnp.zeros_like(values)
    for other_member in range(members):
        difference = values - values[other_member][None]
        magnitude = smooth_abs(difference)
        spread_abs = spread_abs + magnitude
        spread_slope = spread_slope + difference / magnitude
    pair_norm = 2.0 * members * (members - 1)
    crps_value = lax.optimization_barrier(jnp.sum(skill_abs, axis=0)) / members - (lax.optimization_barrier(jnp.sum(spread_abs, axis=0)) - members * SMOOTH) / pair_norm
    loss = jnp.sum(area[None, :] * crps_value) / (VARS * GRID)
    field_grad = (area[None, None, :] * (skill_gap / skill_abs - spread_slope / (members - 1))).astype(jnp.bfloat16)
    return (loss, field_grad)
```

```python
import functools
import math

import jax
import jax.numpy as jnp
from jax import lax
from jax.experimental import pallas as pl
from jax.experimental.pallas import tpu as pltpu
from jax.sharding import PartitionSpec as P

HEADS = 16
SMOOTH = 0.25
EPS = 1e-05
BF = jnp.bfloat16
F32 = jnp.float32
AXES = ("member", "space")
NT = (((1,), (1,)), ((), ()))
TN = (((0,), (0,)), ((), ()))
NONE = -1e30


def dot(a, b, dims=(((1,), (0,)), ((), ()))):
    return lax.dot_general(a, b, dims, preferred_element_type=F32)


def round_up(value, unit):
    return -(-value // unit) * unit


def chip_cycle(chips):
    rows = 1
    while rows * rows * 4 <= chips:
        rows *= 2
    if rows == 1 and chips > 2:
        rows = 2
    depth = chips // rows
    if rows * depth != chips or rows == 1:
        return list(range(chips))
    walk = []
    for y in range(rows):
        zs = range(1, depth) if y % 2 == 0 else range(depth - 1, 0, -1)
        walk += [z * rows + y for z in zs]
    return walk + [y for y in range(rows - 1, -1, -1)]


class Links:
    def __init__(self, members, space):
        self.members, self.space = members, space
        self.chips = space // 2
        self.cycle = chip_cycle(self.chips)
        self.place = [0] * self.chips
        for at, chip in enumerate(self.cycle):
            self.place[chip] = at

    def pairs(self, target):
        out = []
        for m in range(self.members):
            for s in range(self.space):
                tm, ts = target(m, s)
                out.append((m * self.space + s, tm * self.space + ts))
        return out

    def ring(self):
        def target(m, s):
            chip, core = divmod(s, 2)
            step = 1 if core == 0 else -1
            return m, 2 * self.cycle[(self.place[chip] + step) % self.chips] + core

        return self.pairs(target)

    def partner(self):
        return self.pairs(lambda m, s: (m, s ^ 1))

    def outer_halo(self):
        return self.pairs(lambda m, s: (m, (s + (1 if s % 2 else -1)) % self.space))

    def member_shift(self, shift):
        return self.pairs(lambda m, s: ((m - shift) % self.members, s))

    def space_flip(self, bit):
        return self.pairs(lambda m, s: (m, s ^ bit))

    def member_flip(self, bit):
        return self.pairs(lambda m, s: (m ^ bit, s))


def send(x, pairs):
    return lax.ppermute(x, AXES, pairs)


VM = pl.BlockSpec(memory_space=pltpu.VMEM)
SM = pl.BlockSpec(memory_space=pltpu.SMEM)
ANY = pl.BlockSpec(memory_space=pl.ANY)


def start_kernel(where, wq, wk, wv, wo, wd, states, noise, rows, pack, outer, inner):
    m, c = where[0], where[1]
    width = pack.shape[1] - wide(wd.shape[0])
    third = width // 3
    mine = pl.ds(pl.multiple_of(m * third, 128), third)
    for at, ref in enumerate((wq, wk, wv)):
        pack[:, at * third : (at + 1) * third] = ref[:, mine]
    folded = dot(wo[...], wd[...], NT)
    pad = wide(wd.shape[0]) - wd.shape[0]
    folded = jnp.concatenate([folded, jnp.zeros((folded.shape[0], pad), F32)], axis=1)
    pack[:, width:] = folded.astype(BF)
    halo = rows.shape[1] // 2
    nodes = states.shape[0]
    numbers = lax.broadcasted_iota(jnp.int32, (nodes, halo), 0)
    low, high = rows[:, :halo], rows[:, halo:]
    for ref, first in ((outer, c == 0), (inner, c != 0)):
        picked = jnp.where(first, low, high)
        chosen = (numbers == picked).astype(F32).astype(BF)
        if ref.shape[1] == states.shape[1]:
            source = states[...]
        else:
            source = states[:, pl.ds(pl.multiple_of(m * ref.shape[1], 128), ref.shape[1])]
        ref[:halo, :] = dot(chosen, source, TN).astype(BF)
        terms = dot(noise[...], chosen).astype(BF)
        if ref.shape[1] > halo:
            rest = jnp.zeros((terms.shape[0], ref.shape[1] - halo), BF)
            terms = jnp.concatenate([terms, rest], axis=1)
        ref[halo:, :] = terms


def wide(count):
    return round_up(count, 128)


def prepare_kernel(where, edges, states, wd, sources, weights, bias, base, upper, lower):
    c = where[1]
    nodes = states.shape[0]
    total = bias.shape[1]
    halo = (total - nodes) // 2
    e = edges[...]
    turned = jnp.where(e < halo, e + (nodes + halo), jnp.where(e >= nodes + halo, e - (nodes + halo), e))
    e = jnp.where(c == 0, e, turned)
    numbers = lax.broadcasted_iota(jnp.int32, (total, nodes), 0)
    count = jnp.zeros((total, nodes), F32)
    for k in range(e.shape[0]):
        count = count + (numbers == e[k : k + 1, :]).astype(F32)
    logs = jnp.where(count > 0, jnp.log2(jnp.maximum(count, 1.0)), NONE)
    bias[...] = logs.T
    fields = dot(wd[...], states[...], NT)
    pad = base.shape[0] - fields.shape[0]
    base[...] = jnp.concatenate([fields, jnp.zeros((pad, nodes), F32)], axis=0)
    grid = sources.shape[1]
    step = min(grid, 512)
    for at in range(0, grid, step):
        cut = slice(at, at + step)
        numbers = lax.broadcasted_iota(jnp.int32, (nodes, step), 0)
        matrix = jnp.zeros((nodes, step), F32)
        for k in range(sources.shape[0]):
            hit = numbers == sources[k : k + 1, cut]
            matrix = matrix + jnp.where(hit, weights[k : k + 1, cut], 0.0)
        high = matrix.astype(BF)
        upper[:, cut] = high
        lower[:, cut] = (matrix - high.astype(F32)).astype(BF)


def hidden_kernel(where, states, outer, crossed, inner, noise, gain, cond, hidden, values):
    m = where[0]
    members = hidden.shape[0]
    nodes = states.shape[0]
    halo = (hidden.shape[1] - nodes) // 2
    part = outer.shape[1]
    for k in range(members):
        owner = lax.rem(m + k, members)
        source = outer[:halo, :] if k == 0 else crossed[k - 1]
        values[:halo, pl.ds(pl.multiple_of(owner * part, 128), part)] = source.astype(F32)
    values[halo : halo + nodes, :] = states[...].astype(F32)
    values[halo + nodes :, :] = inner[:halo, :].astype(F32)
    width = states.shape[1]
    for at in range(0, hidden.shape[1], 128):
        cut = slice(at, at + 128)
        x = values[cut, :]
        center = x - jnp.mean(x, axis=1, keepdims=True)
        spread = jnp.mean(center * center, axis=1, keepdims=True)
        normed = center * lax.rsqrt(spread + EPS) * gain[...]
        for k in range(members):
            terms = dot(noise[k, :, cut], cond[...], TN)
            hidden[k, cut, :] = (normed * (1.0 + terms[:, :width]) + terms[:, width:]).astype(BF)


def attend_kernel(halves, where, places, hidden, bias, *rest):
    pieces = rest[: len(halves)]
    out, weights, attended, sems = rest[len(halves) :]
    m = where[0]
    step = pl.program_id(0)
    rows = pieces[0].shape[0] // halves[0]

    def copies():
        at = 0
        for ref, count in zip(pieces, halves):
            for half in range(count):
                row = pl.multiple_of(places[at] * rows, rows)
                yield pltpu.make_async_copy(
                    ref.at[pl.ds(half * rows, rows), :], weights.at[pl.ds(row, rows), :], sems.at[at]
                )
                at += 1

    @pl.when(step == 0)
    def _():
        for copy in copies():
            copy.start()
        for copy in copies():
            copy.wait()

    nodes = bias.shape[0]
    total = hidden.shape[1]
    halo = (total - nodes) // 2
    model = hidden.shape[2]
    head = model // HEADS
    third = attended.shape[1]
    scale = math.log2(math.e) / math.sqrt(head)
    every = hidden[0]
    own = hidden[0, halo : halo + nodes, :]
    query = (dot(own, weights[:, :third]) * scale).astype(BF)
    key = dot(every, weights[:, third : 2 * third]).astype(BF)
    value = dot(every, weights[:, 2 * third : 3 * third]).astype(BF)
    group = 128
    lanes = lax.broadcasted_iota(jnp.int32, (nodes, group), 1)
    ones = jnp.ones((total, 128), BF)
    for at in range(0, third, group):
        cut = slice(at, at + group)
        q, k = query[:, cut], key[:, cut]
        v = jnp.concatenate([value[:, cut], ones], axis=1)
        result = None
        for first in range(0, group, head):
            inside = (lanes >= first) & (lanes < first + head)
            masked = jnp.where(inside, q, jnp.zeros_like(q))
            scores = dot(masked, k, NT) + bias[...]
            both = dot(jnp.exp2(scores).astype(BF), v)
            normal = both[:, :group] / both[:, group:]
            result = normal if result is None else jnp.where(inside, normal, result)
        attended[:, cut] = result.astype(BF)
    mine = weights[pl.ds(pl.multiple_of(m * third, 128), third), 3 * third :]
    partial = dot(attended[...], mine)
    out[0] = partial.T[: out.shape[1], :].astype(BF)


def score_kernel(own, others, base, upper, lower, truth, area, grads, loss):
    members, _, _ = own.shape
    variables, grid = truth.shape
    fields = []
    for k in range(members):
        total = own[k].astype(F32)
        for j in range(members - 1):
            total = total + others[j, (k - (j + 1)) % members].astype(F32)
        total = total + base[...]
        high = total.astype(BF)
        low = (total - high.astype(F32)).astype(BF)
        x = dot(high, upper[...]) + (dot(low, upper[...]) + dot(high, lower[...]))
        fields.append(x[:variables].astype(BF).astype(F32))
    y = truth[...].astype(F32)
    weight = area[...]

    def both(d):
        square = d * d + SMOOTH * SMOOTH
        inverse = lax.rsqrt(square)
        return square * inverse, d * inverse

    skill = spread = None
    for k in range(members):
        size, slope = both(fields[k] - y)
        skill = size if skill is None else skill + size
        if k == 0:
            gradient = slope
    pull = None
    for k in range(members):
        for j in range(k + 1, members):
            size, slope = both(fields[k] - fields[j])
            spread = size if spread is None else spread + size
            if k == 0:
                pull = slope if pull is None else pull + slope
    gradient = gradient - pull * (1.0 / (members - 1))
    grads[0] = (weight * gradient).astype(BF)
    crps = skill * (1.0 / members) - spread * (1.0 / (members * (members - 1)))
    summed = jnp.sum(jnp.sum(weight * crps, axis=0, keepdims=True), axis=1, keepdims=True)
    loss[...] = jnp.broadcast_to(summed, loss.shape)


def params(megabytes=32):
    return pltpu.CompilerParams(vmem_limit_bytes=megabytes << 20)


def per_device(
    links,
    node_states,
    noise,
    norm_gain,
    cond_weight,
    w_query,
    w_key,
    w_value,
    w_out,
    edge_src,
    send_rows,
    dec_src,
    dec_weight,
    w_decode,
    truth,
    area,
):
    shape = jax.ShapeDtypeStruct
    members, space = links.members, links.space
    m, s = lax.axis_index("member"), lax.axis_index("space")
    chip, core = s // 2, s % 2
    nodes, model = node_states.shape
    rows = w_query.shape[0]
    third = model // members
    variables, grid = truth.shape
    halo = send_rows.shape[0] // 2
    total = nodes + 2 * halo
    channels = noise.shape[1]
    packed = 3 * third + wide(variables)
    tall = round_up(variables, 16)
    where = jnp.stack([m, core]).astype(jnp.int32)
    own_noise = noise[0]

    shard, outer_out, inner_out = pl.pallas_call(
        start_kernel,
        out_shape=(
            shape((rows, packed), BF),
            shape((halo + channels, third), BF),
            shape((halo + channels, model), BF),
        ),
        in_specs=[SM] + [VM] * 8,
        out_specs=(VM, VM, VM),
        compiler_params=params(),
        name="start",
    )(where, w_query, w_key, w_value, w_out, w_decode, node_states, own_noise, send_rows[None, :])

    partner, ring = links.partner(), links.ring()
    other = send(shard, partner)
    place = jnp.asarray(links.place, jnp.int32)[chip]
    cycle = jnp.asarray(links.cycle, jnp.int32)
    turn = jnp.where(core == 0, -1, 1)
    pieces, halves, order = [shard, other], [1, 1], [s, s ^ 1]
    current = jnp.concatenate([shard, other], axis=0)
    rounds = links.chips // 2
    for r in range(1, rounds + 1):
        last = r == rounds and links.chips % 2 == 0
        current = send(current[:rows] if last else current, ring)
        passed = send(current, partner)
        near = 2 * cycle[(place + turn * r) % links.chips]
        far = 2 * cycle[(place - turn * r) % links.chips]
        pieces += [current, passed]
        if last:
            halves += [1, 1]
            order += [near + core, far + 1 - core]
        else:
            halves += [2, 2]
            order += [near + core, near + 1 - core, far + 1 - core, far + core]

    outer_in = send(outer_out, links.outer_halo())
    inner_in = send(inner_out, partner)
    terms = jnp.concatenate([outer_in[halo:, :halo], own_noise, inner_in[halo:, :halo]], axis=1)
    if third == total:
        message = jnp.concatenate([outer_in[:halo], terms], axis=0)
        crossed = [send(message, links.member_shift(k)) for k in range(1, members)]
        crossed_states = jnp.stack([x[:halo] for x in crossed])
        crossed_terms = [x[halo:] for x in crossed]
    else:
        crossed_states = jnp.stack(
            [send(outer_in[:halo], links.member_shift(k)) for k in range(1, members)]
        )
        crossed_terms = [send(terms, links.member_shift(k)) for k in range(1, members)]
    all_terms = jnp.stack([terms] + crossed_terms)

    bias, base, upper, lower = pl.pallas_call(
        prepare_kernel,
        out_shape=(
            shape((nodes, total), F32),
            shape((tall, nodes), F32),
            shape((nodes, grid), BF),
            shape((nodes, grid), BF),
        ),
        in_specs=[SM] + [VM] * 5,
        out_specs=(VM,) * 4,
        compiler_params=params(),
        name="prepare",
    )(where, edge_src, node_states, w_decode, dec_src, dec_weight)

    hidden = pl.pallas_call(
        hidden_kernel,
        out_shape=shape((members, total, model), BF),
        in_specs=[SM] + [VM] * 7,
        out_specs=VM,
        scratch_shapes=[pltpu.VMEM((total, model), F32)],
        compiler_params=params(),
        name="hidden",
    )(where, node_states, outer_in, crossed_states, inner_in, all_terms, norm_gain[None, :], cond_weight)

    partial = pl.pallas_call(
        functools.partial(attend_kernel, tuple(halves)),
        out_shape=shape((members, tall, nodes), BF),
        grid_spec=pltpu.PrefetchScalarGridSpec(
            num_scalar_prefetch=2,
            grid=(members,),
            in_specs=[
                pl.BlockSpec((1, total, model), lambda i, *_: (i, 0, 0)),
                pl.BlockSpec((nodes, total), lambda i, *_: (0, 0)),
            ]
            + [ANY] * len(pieces),
            out_specs=pl.BlockSpec((1, tall, nodes), lambda i, *_: (i, 0, 0)),
            scratch_shapes=[
                pltpu.VMEM((model, packed), BF),
                pltpu.VMEM((nodes, third), BF),
                pltpu.SemaphoreType.DMA((sum(halves),)),
            ],
        ),
        compiler_params=params(),
        name="attend",
    )(where, jnp.stack(order).astype(jnp.int32), hidden, bias, *pieces)

    others = jnp.stack([send(partial, links.member_shift(k)) for k in range(1, members)])
    field_grad, loss = pl.pallas_call(
        score_kernel,
        out_shape=(shape((1, variables, grid), BF), shape((8, 128), F32)),
        in_specs=[VM] * 7,
        out_specs=(VM, VM),
        compiler_params=params(),
        name="score",
    )(partial, others, base, upper, lower, truth, area[None, :])

    bit = 1
    while bit < space:
        loss = loss + send(loss, links.space_flip(bit))
        bit *= 2
    if members > 2:
        bit = 1
        while bit < members:
            loss = loss + send(loss, links.member_flip(bit))
            bit *= 2
        loss = loss * (1.0 / members)
    loss = loss[0, 0] / (variables * grid * space)
    return (loss, field_grad)


def solution(mesh):
    in_specs = (
        P("space", None),
        P("member", None, "space"),
        P(),
        P(),
        P("space", None),
        P("space", None),
        P("space", None),
        P("space", None),
        P(None, "space"),
        P("space"),
        P(None, "space"),
        P(None, "space"),
        P(),
        P(None, "space"),
        P("space"),
    )
    out_specs = (P(), P("member", None, "space"))
    links = Links(mesh.shape["member"], mesh.shape["space"])
    return jax.shard_map(
        functools.partial(per_device, links),
        mesh=mesh,
        in_specs=in_specs,
        out_specs=out_specs,
        check_vma=False,
    )
```
